128 devices in a mesh: mat: 8 (over z, core), pts: 16 (over y, x).
Axes of the slice: x: 4, y: 4, z: 4, core: 2. Of those that a mesh axis runs over, the one named last changes fastest.
Arguments:
- basis_values: bfloat16 [512, 2048, 512], P(('mat', 'pts')), may hold values from -6 to 6
- tile_ids: int32 [512, 4], P(('mat', 'pts')), may hold values from 0 to 7, as said below
- density_matrix: bfloat16 [1024, 1024], P('mat'), may hold values from -0.01171875 to 0.01171875
- descriptors: bfloat16 [512, 2048, 64], P(('mat', 'pts')), may hold values from -6 to 6
- grid_weights: float32 [512, 2048], P(('mat', 'pts')), may hold values from 0.25 to 2
- centre_ids: int32 [512, 2048], P(('mat', 'pts')), may hold values from 0 to 255
- density_scale: float32 [64], replicated, may hold values from -4 to 4
- norm_gain: float32 [64], replicated, may hold values from 0.1 to 1.9
- w_first: bfloat16 [64, 256], replicated, may hold values from -0.75 to 0.75
- b_first: float32 [256], replicated, may hold values from -3 to 3
- w_second: bfloat16 [256, 256], replicated, may hold values from -0.375 to 0.375
- b_second: float32 [256], replicated, may hold values from -3 to 3
- w_third: bfloat16 [256, 64], replicated, may hold values from -0.375 to 0.375
- b_third: float32 [64], replicated, may hold values from -3 to 3
Outputs:
- potential_matrix: bfloat16 [1024, 1024], P('mat', 'pts')
- centre_features: bfloat16 [256, 64], P('pts')
The draws below stay inside these ranges and needn't reach their ends.
Inputs may be any that keep to these rules, and one draw needn't show every extreme that they name: `tile_ids`: the 4 tiles t of one batch have 4 different values of t.
All inputs are finite; a program needn't handle non-finite values.
Results may differ from the reference program's by a relative error of at most 0.0064.
Values may be sent and summed in bfloat16 or wider, within the bound.
No kernel may reach another device: no remote copies, remote signals or barrier semaphores. Data moves between devices by JAX's collectives and lax.ppermute only.
A program may use at most 64 MiB of HBM per device.

```python
import math
import jax
import jax.numpy as jnp
from jax import lax

ORB = 512
TILE = 128
FEAT = 64
HID = 256
PTS = 2048
BATCHES = 512
KT = 4
TPD = 1
NBAS = 1024
NT = 8
NCENT = 256


def draw_tile_ids(key, part):
    owner_total = NT // TPD
    leading, trailing = jax.random.split(jax.random.fold_in(key, 11))
    scores = jax.random.randint(leading, (BATCHES, owner_total), 0, 1 << 20) * owner_total + jnp.arange(owner_total, dtype=jnp.int32)[None, :]
    owners = jnp.argsort(scores, axis=1)[:, :KT].astype(jnp.int32)
    local_tiles = jax.random.randint(trailing, (BATCHES, KT), 0, TPD).astype(jnp.int32)
    return (owners * TPD + local_tiles).astype(jnp.int32)


def centre_lists(key):
    return jax.random.randint(jax.random.fold_in(key, 23), (BATCHES, PTS), 0, NCENT).astype(jnp.int32)


def draw_centre_ids(key, part):
    return centre_lists(key)


def draw_descriptors(key, part):
    owners = centre_lists(key)
    spread_key, value_key = jax.random.split(jax.random.fold_in(key, 29))
    log_scales = jax.random.uniform(spread_key, (NCENT, FEAT), jnp.float32, math.log(0.3), math.log(3.0))
    values = jax.random.normal(value_key, (BATCHES, PTS, FEAT), jnp.float32)
    scales = jnp.exp(log_scales)[owners]
    return jnp.clip(scales * values, -6.0, 6.0).astype(jnp.bfloat16)


def level_of(own_key, dims, shards, low, largest):
    loudness, own = 1.0, jax.random.fold_in(own_key, 6)
    for position, parts in shards:
        steps = jnp.exp(jax.random.uniform(jax.random.fold_in(own, position), (parts,), jnp.float32, low / len(shards), largest / len(shards)))
        loudness = loudness * jnp.repeat(steps, dims[position] // parts).reshape([-1 if axis == position else 1 for axis in range(len(dims))])
    return loudness


def scatter_about(rng, dims, width, most, pieces=(), kind=jnp.bfloat16):
    array = width * jax.random.normal(rng, dims, jnp.float32)
    if pieces:
        array = array * level_of(rng, dims, pieces, -0.22, 0.18)
    return jnp.clip(array, -most, most).astype(kind)


def setup_inputs(seed: int = 0) -> dict:
    arg_keys = jax.random.split(jax.random.key(seed), 15)
    basis_values = scatter_about(arg_keys[0], (BATCHES, PTS, ORB), 1.0, 6.0, ((0, 128),))
    tile_ids = draw_tile_ids(jax.random.fold_in(arg_keys[14], 71), 0)
    density_matrix = scatter_about(arg_keys[2], (NBAS, NBAS), (ORB * ORB) ** -0.5, 0.01171875, ((0, 8),))
    descriptors = draw_descriptors(jax.random.fold_in(arg_keys[14], 71), 0)
    grid_weights = jnp.clip(jnp.exp(math.log(2.0) - 2.0794415 * jax.random.uniform(arg_keys[4], (BATCHES, PTS), jnp.float32) ** level_of(arg_keys[4], (BATCHES, PTS), ((0, 128),), -0.2, 0.2)), 0.25, 2.0)
    centre_ids = draw_centre_ids(jax.random.fold_in(arg_keys[14], 71), 0)
    density_scale = scatter_about(arg_keys[6], (FEAT,), 1.0, 4.0, (), jnp.float32)
    norm_gain = jnp.clip(1.0 + 0.18 * jax.random.normal(arg_keys[7], (FEAT,), jnp.float32), 0.1, 1.9)
    w_first = scatter_about(arg_keys[8], (FEAT, HID), FEAT ** -0.5, 0.75)
    b_first = scatter_about(arg_keys[9], (HID,), 0.5, 3.0, (), jnp.float32)
    w_second = scatter_about(arg_keys[10], (HID, HID), HID ** -0.5, 0.375)
    b_second = scatter_about(arg_keys[11], (HID,), 0.5, 3.0, (), jnp.float32)
    w_third = scatter_about(arg_keys[12], (HID, FEAT), HID ** -0.5, 0.375)
    b_third = scatter_about(arg_keys[13], (FEAT,), 0.5, 3.0, (), jnp.float32)
    return {"basis_values": basis_values, "tile_ids": tile_ids, "density_matrix": density_matrix, "descriptors": descriptors, "grid_weights": grid_weights, "centre_ids": centre_ids, "density_scale": density_scale, "norm_gain": norm_gain, "w_first": w_first, "b_first": b_first, "w_second": w_second, "b_second": b_second, "w_third": w_third, "b_third": b_third}


def orbital_rows(tile_list):
    offsets = jnp.arange(TILE, dtype=jnp.int32)
    return (tile_list.astype(jnp.int32)[:, None] * TILE + offsets[None, :]).reshape(-1).astype(jnp.int32)

def centre_network(summed, norm_gain, w_first, b_first, w_second, b_second, w_third, b_third):
    inverse = lax.rsqrt(lax.optimization_barrier(jnp.mean(summed * summed, axis=1, keepdims=True)) + 1e-05)
    normed = (summed * inverse * norm_gain).astype(jnp.bfloat16)
    hidden_one = jax.nn.silu(jnp.dot(normed, w_first, preferred_element_type=jnp.float32) + b_first).astype(jnp.bfloat16)
    hidden_two = jax.nn.silu(jnp.dot(hidden_one, w_second, preferred_element_type=jnp.float32) + b_second).astype(jnp.bfloat16)
    return (jnp.dot(hidden_two, w_third, preferred_element_type=jnp.float32) + b_third).astype(jnp.bfloat16)

def reference(basis_values, tile_ids, density_matrix, descriptors, grid_weights, centre_ids, density_scale, norm_gain, w_first, b_first, w_second, b_second, w_third, b_third):

    def batch_density(inputs):
        values, tile_list = inputs
        orbital = orbital_rows(tile_list)
        panel_full = density_matrix[orbital][:, orbital]
        projected = jnp.dot(values, panel_full, preferred_element_type=jnp.float32)
        return lax.optimization_barrier(jnp.sum(values.astype(jnp.float32) * projected, axis=1))
    density = lax.map(batch_density, (basis_values, tile_ids))
    radial_terms = descriptors.astype(jnp.float32)
    features = jax.nn.silu(density[:, :, None] * density_scale + radial_terms)
    weighted_feat = grid_weights[:, :, None] * features
    centre_sum = jax.ops.segment_sum(weighted_feat.reshape(-1, FEAT), centre_ids.reshape(-1), num_segments=NCENT)
    centre_features = centre_network(centre_sum, norm_gain, w_first, b_first, w_second, b_second, w_third, b_third)
    nearest = centre_features[centre_ids].astype(jnp.float32)
    factor = NT / (KT * math.sqrt(PTS * FEAT * BATCHES))
    point_potential = grid_weights * density * lax.optimization_barrier(jnp.sum(nearest * radial_terms, axis=2)) * factor

    def assemble(accumulated, inputs):
        values, tile_list, local_potential = inputs
        orbital = orbital_rows(tile_list)
        weighted = (local_potential[:, None] * values.astype(jnp.float32)).astype(jnp.bfloat16)
        tile_block = jnp.dot(values.T, weighted, preferred_element_type=jnp.float32)
        return (accumulated.at[orbital[:, None], orbital[None, :]].add(tile_block), None)
    accumulated, ignored = lax.scan(assemble, jnp.zeros((NBAS, NBAS), jnp.float32), (basis_values, tile_ids, point_potential))
    return (accumulated.astype(jnp.bfloat16), centre_features)
```

```python
import functools
import math

import jax
import jax.numpy as jnp
from jax import lax
from jax.experimental import pallas as pl
from jax.experimental.pallas import tpu as pltpu
from jax.sharding import PartitionSpec as P

BF = jnp.bfloat16
F32 = jnp.float32
LANES = (((1,), (1,)), ((), ()))
MB = 1 << 20
CENT_DEV = 16


def whole(shape):
    return pl.BlockSpec(shape, lambda *_: (0,) * len(shape))


def in_hbm(x):
    return pltpu.with_memory_space_constraint(x, pltpu.HBM)


def silu(v):
    return v / (1.0 + jnp.exp(-v))


def one_hot(ids_row, centres):
    rows = lax.broadcasted_iota(jnp.int32, (centres, ids_row.shape[1]), 0)
    return (rows == ids_row).astype(F32).astype(BF)


def transpose_kernel(x_ref, o_ref):
    o_ref[0] = x_ref[0].T


def transposed(x, chunk):
    batches, points, orbitals = x.shape
    return pl.pallas_call(
        transpose_kernel,
        grid=(batches, points // chunk),
        in_specs=[pl.BlockSpec((1, chunk, orbitals), lambda b, r: (b, r, 0))],
        out_specs=pl.BlockSpec((1, orbitals, chunk), lambda b, r: (b, 0, r)),
        out_shape=jax.ShapeDtypeStruct((batches, orbitals, points), x.dtype),
        compiler_params=pltpu.CompilerParams(vmem_limit_bytes=16 * MB),
        cost_estimate=pl.CostEstimate(
            flops=0, bytes_accessed=4 * x.size, transcendentals=0
        ),
    )(in_hbm(x))


def sum_kernel(x_ref, o_ref):
    total = jnp.sum(x_ref[...].astype(F32), axis=0).astype(o_ref.dtype)
    o_ref[...] = jnp.broadcast_to(total, o_ref.shape)


def summed(x, copies=()):
    return pl.pallas_call(
        sum_kernel,
        out_shape=jax.ShapeDtypeStruct((*copies, *x.shape[1:]), x.dtype),
        compiler_params=pltpu.CompilerParams(vmem_limit_bytes=8 * MB),
    )(x)


def slab_copies(pos_ref, chips, slabs, table_ref, sem_ref):
    core, z = pos_ref[0], pos_ref[2]
    half = table_ref.shape[1] // 2
    top, bottom = pl.ds(0, half), pl.ds(half, half)
    every = pl.ds(0, 2 * half)
    places = [(0, every), (chips - 1, every), (1, every), (2, top), (2, bottom)]
    copies = []
    for side in range(2):
        for k, (shift, rows) in enumerate(places):
            chip = lax.rem(z + shift, chips)
            slot = 2 * chip + (core if side == 0 else 1 - core)
            n = side * len(places) + k
            copies.append(
                pltpu.make_async_copy(slabs[n], table_ref.at[slot, rows], sem_ref.at[n])
            )
    return copies


def density_kernel(
    tile, chunk, chips, tid_ref, pos_ref, *refs
):
    slabs, refs = refs[:10], refs[10:]
    density_body(tile, chunk, chips, tid_ref, pos_ref, slabs, *refs)


def density_body(
    tile, chunk, chips, tid_ref, pos_ref, slabs, xt_ref, desc_ref, w_ref, ids_ref, scale_ref,
    dens_ref, sum_ref, table_ref, panel_ref, acc_ref, sem_ref,
):
    b, part = pl.program_id(0), pl.program_id(1)
    parts = pl.num_programs(1)
    orbitals, points = xt_ref.shape[1:]
    per_batch = orbitals // tile
    feats = desc_ref.shape[1]
    centres = sum_ref.shape[2]

    @pl.when((b == 0) & (part == 0))
    def _():
        copies = slab_copies(pos_ref, chips, slabs, table_ref, sem_ref)
        for copy in copies:
            copy.start()
        for copy in copies:
            copy.wait()

    @pl.when(part == 0)
    def _():
        for i in range(per_batch):
            ti = tid_ref[b, i]
            for j in range(per_batch):
                tj = tid_ref[b, j]
                panel_ref[i * tile : (i + 1) * tile, j * tile : (j + 1) * tile] = table_ref[
                    ti, :, pl.ds(pl.multiple_of(tj * tile, tile), tile)
                ]

    gathered = jnp.zeros(acc_ref.shape[1:], F32)
    for r in range(points // chunk):
        at = slice(r * chunk, (r + 1) * chunk)
        out = pl.ds(pl.multiple_of(part * points + r * chunk, chunk), chunk)
        xt = xt_ref[0, :, at]
        q = jnp.dot(panel_ref[...], xt, preferred_element_type=F32)
        dens = jnp.sum(xt.astype(F32) * q, axis=0, keepdims=True)
        dens_ref[pl.ds(b, 1), out] = dens
        f = silu(dens * scale_ref[...] + desc_ref[0, :, at].astype(F32))
        f = f * w_ref[pl.ds(b, 1), out]
        high = f.astype(BF)
        low = (f - high.astype(F32)).astype(BF)
        both = jnp.concatenate([high, low], axis=0)
        hot = one_hot(ids_ref[pl.ds(b, 1), out], centres)
        gathered += lax.dot_general(both, hot, LANES, preferred_element_type=F32)
    acc_ref[b * parts + part] = gathered

    @pl.when((b == pl.num_programs(0) - 1) & (part == parts - 1))
    def _():
        total = jnp.sum(acc_ref[...], axis=0)
        total = (total[:feats] + total[feats:]).astype(sum_ref.dtype)
        sum_ref[...] = jnp.broadcast_to(total, sum_ref.shape)


def potential_kernel(
    tile, chunk, factor, tid_ref, pos_ref, sums_ref, gain_ref, w1_ref, b1_ref, w2_ref, b2_ref, w3_ref,
    b3_ref, dens_ref, desc_ref, w_ref, ids_ref, xt_ref, x_ref, own_ref, other_ref, cf_ref,
    cft_ref, cfall_ref, wt_ref, acc_ref,
):
    b = pl.program_id(0)
    orbitals, points = xt_ref.shape[1:]
    per_batch = orbitals // tile
    centres = cft_ref.shape[1]
    mine = cf_ref.shape[0]

    @pl.when(b == 0)
    def _():
        acc_ref[...] = jnp.zeros_like(acc_ref)
        total = jnp.sum(sums_ref[...].astype(F32), axis=0)
        inverse = lax.rsqrt(jnp.mean(total * total, axis=0, keepdims=True) + 1e-05)
        normed = ((total * inverse).T * gain_ref[...]).astype(BF)
        one = silu(
            jnp.dot(normed, w1_ref[...], preferred_element_type=F32) + b1_ref[...]
        ).astype(BF)
        two = silu(
            jnp.dot(one, w2_ref[...], preferred_element_type=F32) + b2_ref[...]
        ).astype(BF)
        feats = lax.dot_general(two, w3_ref[...], LANES, preferred_element_type=F32) + b3_ref[...]
        cfall_ref[...] = feats
        cf_ref[...] = cfall_ref[pl.ds(pl.multiple_of(pos_ref[1] * mine, 8), mine), :].astype(BF)
        cft_ref[...] = feats.T.astype(BF)

    for r in range(points // chunk):
        at = slice(r * chunk, (r + 1) * chunk)
        hot = one_hot(ids_ref[pl.ds(b, 1), at], centres)
        nearest = jnp.dot(cft_ref[...], hot, preferred_element_type=F32)
        inner = jnp.sum(nearest * desc_ref[0, :, at].astype(F32), axis=0, keepdims=True)
        v = w_ref[pl.ds(b, 1), at] * dens_ref[pl.ds(b, 1), at] * inner * factor
        wt_ref[:, at] = (v * xt_ref[0, :, at].astype(F32)).astype(BF)
    for i in range(per_batch):
        rows = slice(i * tile, (i + 1) * tile)
        block = jnp.dot(wt_ref[rows, :], x_ref[0], preferred_element_type=F32)
        for j in range(per_batch):
            acc_ref[tid_ref[b, i], tid_ref[b, j]] += block[:, j * tile : (j + 1) * tile]

    @pl.when(b == pl.num_programs(0) - 1)
    def _():
        core = pos_ref[0]
        for z in range(own_ref.shape[0]):
            for i in range(own_ref.shape[1]):
                own_ref[z, i] = acc_ref[i, 2 * z + core]
                other_ref[z, i] = acc_ref[i, 2 * z + 1 - core].astype(BF)


def shards(
    basis_values, tile_ids, density_matrix, descriptors, grid_weights, centre_ids, density_scale,
    norm_gain, w_first, b_first, w_second, b_second, w_third, b_third,
):
    batches, points, orbitals = basis_values.shape
    per_batch = tile_ids.shape[1]
    tile = orbitals // per_batch
    basis = density_matrix.shape[1]
    tiles = basis // tile
    feats = descriptors.shape[2]
    mats = lax.axis_size("mat")
    columns = lax.axis_size("pts")
    chips = mats // 2
    mine = CENT_DEV
    centres = mine * columns
    chunk = 512
    parts = 1
    here, there = lax.axis_index("mat"), lax.axis_index("pts")
    pos = jnp.stack([here % 2, there, here // 2]).astype(jnp.int32)
    swap = [(i, i ^ 1) for i in range(mats)]
    up = [(i, (i + 2) % mats) for i in range(mats)]
    down = [(i, (i - 2) % mats) for i in range(mats)]
    across = [(i, (i + 4) % mats) for i in range(mats)]
    same_core = [
        [m * columns + p for m in range(c, mats, 2) for p in range(columns)] for c in range(2)
    ]
    desc = jnp.swapaxes(descriptors, 1, 2)
    scale = density_scale.reshape(feats, 1)

    top = lax.ppermute(density_matrix[: tile // 2], "mat", across)
    bottom = lax.ppermute(density_matrix[tile // 2 :], "mat", across)
    below = lax.ppermute(density_matrix, "mat", up)
    above = lax.ppermute(density_matrix, "mat", down)
    xt = transposed(basis_values, points)
    top, bottom, below, above, xt = lax.optimization_barrier((top, bottom, below, above, xt))
    slabs = [density_matrix, below, above, top, bottom]
    slabs += [lax.ppermute(slab, "mat", swap) for slab in slabs]

    density, partial = pl.pallas_call(
        functools.partial(density_kernel, tile, chunk, chips),
        grid_spec=pltpu.PrefetchScalarGridSpec(
            num_scalar_prefetch=2,
            grid=(batches, parts),
            in_specs=[
                *[pl.BlockSpec(memory_space=pl.ANY)] * len(slabs),
                pl.BlockSpec((1, orbitals, points // parts), lambda b, r, *_: (b, 0, r)),
                pl.BlockSpec((1, feats, points // parts), lambda b, r, *_: (b, 0, r)),
                whole((batches, points)),
                whole((batches, points)),
                whole((feats, 1)),
            ],
            out_specs=[whole((batches, points)), whole((mats, feats, centres))],
            scratch_shapes=[
                pltpu.VMEM((tiles, tile, basis), BF),
                pltpu.VMEM((orbitals, orbitals), BF),
                pltpu.VMEM((batches * parts, 2 * feats, centres), F32),
                pltpu.SemaphoreType.DMA((len(slabs),)),
            ],
        ),
        out_shape=[
            jax.ShapeDtypeStruct((batches, points), F32),
            jax.ShapeDtypeStruct((mats, feats, centres), BF),
        ],
        compiler_params=pltpu.CompilerParams(vmem_limit_bytes=16 * MB),
        cost_estimate=pl.CostEstimate(
            flops=2 * batches * points * orbitals * orbitals,
            bytes_accessed=2 * basis_values.size,
            transcendentals=descriptors.size,
        ),
    )(tile_ids, pos, *slabs, in_hbm(xt), desc, grid_weights, centre_ids, scale)

    first = summed(lax.all_to_all(partial, "mat", 0, 0, tiled=True), (columns,))
    sums = lax.all_to_all(first, "pts", 0, 0, tiled=True)

    all_batches = batches * mats * columns
    factor = tiles / (per_batch * math.sqrt(points * feats * all_batches))
    hidden = w_first.shape[1]
    own, other, centre_features = pl.pallas_call(
        functools.partial(potential_kernel, tile, chunk, factor),
        grid_spec=pltpu.PrefetchScalarGridSpec(
            num_scalar_prefetch=2,
            grid=(batches,),
            in_specs=[
                whole((columns, feats, centres)),
                whole((1, feats)),
                whole((feats, hidden)),
                whole((1, hidden)),
                whole((hidden, hidden)),
                whole((1, hidden)),
                whole((feats, hidden)),
                whole((1, feats)),
                whole((batches, points)),
                pl.BlockSpec((1, feats, points), lambda b, *_: (b, 0, 0)),
                whole((batches, points)),
                whole((batches, points)),
                pl.BlockSpec((1, orbitals, points), lambda b, *_: (b, 0, 0)),
                pl.BlockSpec((1, points, orbitals), lambda b, *_: (b, 0, 0)),
            ],
            out_specs=[
                whole((chips, tiles, tile, tile)),
                whole((chips, tiles, tile, tile)),
                whole((mine, feats)),
            ],
            scratch_shapes=[
                pltpu.VMEM((feats, centres), BF),
                pltpu.VMEM((centres, feats), F32),
                pltpu.VMEM((orbitals, points), BF),
                pltpu.VMEM((tiles, tiles, tile, tile), F32),
            ],
        ),
        out_shape=[
            jax.ShapeDtypeStruct((chips, tiles, tile, tile), F32),
            jax.ShapeDtypeStruct((chips, tiles, tile, tile), BF),
            jax.ShapeDtypeStruct((mine, feats), BF),
        ],
        compiler_params=pltpu.CompilerParams(vmem_limit_bytes=28 * MB),
        cost_estimate=pl.CostEstimate(
            flops=2 * batches * points * orbitals * orbitals,
            bytes_accessed=4 * basis_values.size,
            transcendentals=2 * centres * hidden,
        ),
    )(
        tile_ids, pos, sums, norm_gain.reshape(1, feats), w_first, b_first.reshape(1, hidden),
        w_second, b_second.reshape(1, hidden), w_third.T, b_third.reshape(1, feats), density, desc,
        grid_weights, centre_ids, xt, basis_values,
    )

    joined = (own + lax.ppermute(other, "mat", swap).astype(F32)).astype(BF)
    joined = joined.reshape(chips * columns, basis // columns, tile)
    pieces = lax.all_to_all(
        joined, ("mat", "pts"), 0, 0, tiled=True, axis_index_groups=same_core
    )
    return (summed(pieces).T, centre_features)


def solution(mesh):
    return jax.shard_map(
        shards,
        mesh=mesh,
        in_specs=(
            P(("mat", "pts"), None, None),
            P(("mat", "pts"), None),
            P("mat", None),
            P(("mat", "pts"), None, None),
            P(("mat", "pts"), None),
            P(("mat", "pts"), None),
            P(), P(), P(), P(), P(), P(), P(), P(),
        ),
        out_specs=(P("mat", "pts"), P("pts", None)),
        check_vma=False,
    )
```

```python
import functools
import math

import jax
import jax.numpy as jnp
from jax import lax
from jax.experimental import pallas as pl
from jax.experimental.pallas import tpu as pltpu
from jax.sharding import PartitionSpec as P

BF = jnp.bfloat16
F32 = jnp.float32
LANES = (((1,), (1,)), ((), ()))
MB = 1 << 20
CENT_DEV = 16


def whole(shape):
    return pl.BlockSpec(shape, lambda *_: (0,) * len(shape))


def in_hbm(x):
    return pltpu.with_memory_space_constraint(x, pltpu.HBM)


def silu(v):
    return v / (1.0 + jnp.exp(-v))


def one_hot(ids_row, centres):
    rows = lax.broadcasted_iota(jnp.int32, (centres, ids_row.shape[1]), 0)
    return (rows == ids_row).astype(F32).astype(BF)


def transpose_kernel(x_ref, o_ref):
    o_ref[0] = x_ref[0].T


def transposed(x, chunk):
    batches, points, orbitals = x.shape
    return pl.pallas_call(
        transpose_kernel,
        grid=(batches, points // chunk),
        in_specs=[pl.BlockSpec((1, chunk, orbitals), lambda b, r: (b, r, 0))],
        out_specs=pl.BlockSpec((1, orbitals, chunk), lambda b, r: (b, 0, r)),
        out_shape=jax.ShapeDtypeStruct((batches, orbitals, points), x.dtype),
        compiler_params=pltpu.CompilerParams(vmem_limit_bytes=16 * MB),
        cost_estimate=pl.CostEstimate(
            flops=0, bytes_accessed=4 * x.size, transcendentals=0
        ),
    )(in_hbm(x))


def sum_kernel(x_ref, o_ref):
    total = jnp.sum(x_ref[...].astype(F32), axis=0).astype(o_ref.dtype)
    o_ref[...] = jnp.broadcast_to(total, o_ref.shape)


def summed(x, copies=()):
    return pl.pallas_call(
        sum_kernel,
        out_shape=jax.ShapeDtypeStruct((*copies, *x.shape[1:]), x.dtype),
        compiler_params=pltpu.CompilerParams(vmem_limit_bytes=8 * MB),
    )(x)


def place_slabs(pos_ref, chips, slabs, table_ref):
    core, z = pos_ref[0], pos_ref[2]
    half = table_ref.shape[1] // 2
    places = [(0, 0), (chips - 1, 0), (1, 0), (2, 0), (2, half)]
    for side in range(2):
        for k, (shift, start) in enumerate(places):
            slot = 2 * lax.rem(z + shift, chips) + (core if side == 0 else 1 - core)
            slab = slabs[side * len(places) + k]
            table_ref[slot, start : start + slab.shape[0], :] = slab[...]


def density_kernel(
    tile, chunk, chips, tid_ref, pos_ref, *refs
):
    slabs, refs = refs[:10], refs[10:]
    density_body(tile, chunk, chips, tid_ref, pos_ref, slabs, *refs)


def density_body(
    tile, chunk, chips, tid_ref, pos_ref, slabs, x_ref, desc_ref, w_ref, ids_ref, scale_ref,
    dens_ref, sum_ref, table_ref, panel_ref, acc_ref,
):
    b = pl.program_id(0)
    points, orbitals = x_ref.shape[1:]
    per_batch = orbitals // tile
    feats = desc_ref.shape[1]
    centres = sum_ref.shape[2]

    @pl.when(b == 0)
    def _():
        place_slabs(pos_ref, chips, slabs, table_ref)

    for i in range(per_batch):
        ti = tid_ref[b, i]
        for j in range(per_batch):
            tj = tid_ref[b, j]
            panel_ref[i * tile : (i + 1) * tile, j * tile : (j + 1) * tile] = table_ref[
                ti, :, pl.ds(pl.multiple_of(tj * tile, tile), tile)
            ]

    gathered = jnp.zeros(acc_ref.shape[1:], F32)
    for r in range(points // chunk):
        at = slice(r * chunk, (r + 1) * chunk)
        xt = x_ref[0, at, :].T
        q = jnp.dot(panel_ref[...], xt, preferred_element_type=F32)
        dens = jnp.sum(xt.astype(F32) * q, axis=0, keepdims=True)
        dens_ref[pl.ds(b, 1), at] = dens
        f = silu(dens * scale_ref[...] + desc_ref[0, :, at].astype(F32))
        f = f * w_ref[pl.ds(b, 1), at]
        high = f.astype(BF)
        low = (f - high.astype(F32)).astype(BF)
        both = jnp.concatenate([high, low], axis=0)
        hot = one_hot(ids_ref[pl.ds(b, 1), at], centres)
        gathered += lax.dot_general(both, hot, LANES, preferred_element_type=F32)
    acc_ref[b] = gathered

    @pl.when(b == pl.num_programs(0) - 1)
    def _():
        total = jnp.sum(acc_ref[...], axis=0)
        total = (total[:feats] + total[feats:]).astype(sum_ref.dtype)
        sum_ref[...] = jnp.broadcast_to(total, sum_ref.shape)


def potential_kernel(
    tile, chunk, factor, tid_ref, pos_ref, sums_ref, gain_ref, w1_ref, b1_ref, w2_ref, b2_ref, w3_ref,
    b3_ref, dens_ref, desc_ref, w_ref, ids_ref, xt_ref, x_ref, own_ref, other_ref, cf_ref,
    cft_ref, cfall_ref, wt_ref, acc_ref,
):
    b = pl.program_id(0)
    orbitals, points = xt_ref.shape[1:]
    per_batch = orbitals // tile
    centres = cft_ref.shape[1]
    mine = cf_ref.shape[0]

    @pl.when(b == 0)
    def _():
        acc_ref[...] = jnp.zeros_like(acc_ref)
        total = jnp.sum(sums_ref[...].astype(F32), axis=0)
        inverse = lax.rsqrt(jnp.mean(total * total, axis=0, keepdims=True) + 1e-05)
        normed = ((total * inverse).T * gain_ref[...]).astype(BF)
        one = silu(
            jnp.dot(normed, w1_ref[...], preferred_element_type=F32) + b1_ref[...]
        ).astype(BF)
        two = silu(
            jnp.dot(one, w2_ref[...], preferred_element_type=F32) + b2_ref[...]
        ).astype(BF)
        feats = lax.dot_general(two, w3_ref[...], LANES, preferred_element_type=F32) + b3_ref[...]
        cfall_ref[...] = feats
        cf_ref[...] = cfall_ref[pl.ds(pl.multiple_of(pos_ref[1] * mine, 8), mine), :].astype(BF)
        cft_ref[...] = feats.T.astype(BF)

    for r in range(points // chunk):
        at = slice(r * chunk, (r + 1) * chunk)
        hot = one_hot(ids_ref[pl.ds(b, 1), at], centres)
        nearest = jnp.dot(cft_ref[...], hot, preferred_element_type=F32)
        inner = jnp.sum(nearest * desc_ref[0, :, at].astype(F32), axis=0, keepdims=True)
        v = w_ref[pl.ds(b, 1), at] * dens_ref[pl.ds(b, 1), at] * inner * factor
        wt_ref[:, at] = (v * xt_ref[0, :, at].astype(F32)).astype(BF)
    for i in range(per_batch):
        rows = slice(i * tile, (i + 1) * tile)
        block = jnp.dot(wt_ref[rows, :], x_ref[0], preferred_element_type=F32)
        for j in range(per_batch):
            acc_ref[tid_ref[b, i], tid_ref[b, j]] += block[:, j * tile : (j + 1) * tile]

    @pl.when(b == pl.num_programs(0) - 1)
    def _():
        core = pos_ref[0]
        for z in range(own_ref.shape[0]):
            for i in range(own_ref.shape[1]):
                own_ref[z, i] = acc_ref[i, 2 * z + core]
                other_ref[z, i] = acc_ref[i, 2 * z + 1 - core].astype(BF)


def shards(
    basis_values, tile_ids, density_matrix, descriptors, grid_weights, centre_ids, density_scale,
    norm_gain, w_first, b_first, w_second, b_second, w_third, b_third,
):
    batches, points, orbitals = basis_values.shape
    per_batch = tile_ids.shape[1]
    tile = orbitals // per_batch
    basis = density_matrix.shape[1]
    tiles = basis // tile
    feats = descriptors.shape[2]
    mats = lax.axis_size("mat")
    columns = lax.axis_size("pts")
    chips = mats // 2
    mine = CENT_DEV
    centres = mine * columns
    chunk = 512
    here, there = lax.axis_index("mat"), lax.axis_index("pts")
    pos = jnp.stack([here % 2, there, here // 2]).astype(jnp.int32)
    swap = [(i, i ^ 1) for i in range(mats)]
    up = [(i, (i + 2) % mats) for i in range(mats)]
    down = [(i, (i - 2) % mats) for i in range(mats)]
    across = [(i, (i + 4) % mats) for i in range(mats)]
    same_core = [
        [m * columns + p for m in range(c, mats, 2) for p in range(columns)] for c in range(2)
    ]
    desc = jnp.swapaxes(descriptors, 1, 2)
    scale = density_scale.reshape(feats, 1)

    top = lax.ppermute(density_matrix[: tile // 2], "mat", across)
    bottom = lax.ppermute(density_matrix[tile // 2 :], "mat", across)
    below = lax.ppermute(density_matrix, "mat", up)
    above = lax.ppermute(density_matrix, "mat", down)
    xt = transposed(basis_values, points)
    top, bottom, below, above, xt = lax.optimization_barrier((top, bottom, below, above, xt))
    slabs = [density_matrix, below, above, top, bottom]
    slabs += [lax.ppermute(slab, "mat", swap) for slab in slabs]

    density, partial = pl.pallas_call(
        functools.partial(density_kernel, tile, chunk, chips),
        grid_spec=pltpu.PrefetchScalarGridSpec(
            num_scalar_prefetch=2,
            grid=(batches,),
            in_specs=[
                *[whole(slab.shape) for slab in slabs],
                pl.BlockSpec((1, points, orbitals), lambda b, *_: (b, 0, 0)),
                pl.BlockSpec((1, feats, points), lambda b, *_: (b, 0, 0)),
                whole((batches, points)),
                whole((batches, points)),
                whole((feats, 1)),
            ],
            out_specs=[whole((batches, points)), whole((mats, feats, centres))],
            scratch_shapes=[
                pltpu.VMEM((tiles, tile, basis), BF),
                pltpu.VMEM((orbitals, orbitals), BF),
                pltpu.VMEM((batches, 2 * feats, centres), F32),
            ],
        ),
        out_shape=[
            jax.ShapeDtypeStruct((batches, points), F32),
            jax.ShapeDtypeStruct((mats, feats, centres), BF),
        ],
        compiler_params=pltpu.CompilerParams(vmem_limit_bytes=16 * MB),
        cost_estimate=pl.CostEstimate(
            flops=2 * batches * points * orbitals * orbitals,
            bytes_accessed=2 * basis_values.size,
            transcendentals=descriptors.size,
        ),
    )(
        tile_ids, pos, *slabs, in_hbm(basis_values), desc, grid_weights, centre_ids, scale,
    )

    first = summed(lax.all_to_all(partial, "mat", 0, 0, tiled=True), (columns,))
    sums = lax.all_to_all(first, "pts", 0, 0, tiled=True)

    all_batches = batches * mats * columns
    factor = tiles / (per_batch * math.sqrt(points * feats * all_batches))
    hidden = w_first.shape[1]
    own, other, centre_features = pl.pallas_call(
        functools.partial(potential_kernel, tile, chunk, factor),
        grid_spec=pltpu.PrefetchScalarGridSpec(
            num_scalar_prefetch=2,
            grid=(batches,),
            in_specs=[
                whole((columns, feats, centres)),
                whole((1, feats)),
                whole((feats, hidden)),
                whole((1, hidden)),
                whole((hidden, hidden)),
                whole((1, hidden)),
                whole((feats, hidden)),
                whole((1, feats)),
                whole((batches, points)),
                pl.BlockSpec((1, feats, points), lambda b, *_: (b, 0, 0)),
                whole((batches, points)),
                whole((batches, points)),
                pl.BlockSpec((1, orbitals, points), lambda b, *_: (b, 0, 0)),
                pl.BlockSpec((1, points, orbitals), lambda b, *_: (b, 0, 0)),
            ],
            out_specs=[
                whole((chips, tiles, tile, tile)),
                whole((chips, tiles, tile, tile)),
                whole((mine, feats)),
            ],
            scratch_shapes=[
                pltpu.VMEM((feats, centres), BF),
                pltpu.VMEM((centres, feats), F32),
                pltpu.VMEM((orbitals, points), BF),
                pltpu.VMEM((tiles, tiles, tile, tile), F32),
            ],
        ),
        out_shape=[
            jax.ShapeDtypeStruct((chips, tiles, tile, tile), F32),
            jax.ShapeDtypeStruct((chips, tiles, tile, tile), BF),
            jax.ShapeDtypeStruct((mine, feats), BF),
        ],
        compiler_params=pltpu.CompilerParams(vmem_limit_bytes=28 * MB),
        cost_estimate=pl.CostEstimate(
            flops=2 * batches * points * orbitals * orbitals,
            bytes_accessed=4 * basis_values.size,
            transcendentals=2 * centres * hidden,
        ),
    )(
        tile_ids, pos, sums, norm_gain.reshape(1, feats), w_first, b_first.reshape(1, hidden),
        w_second, b_second.reshape(1, hidden), w_third.T, b_third.reshape(1, feats), density, desc,
        grid_weights, centre_ids, xt, basis_values,
    )

    joined = (own + lax.ppermute(other, "mat", swap).astype(F32)).astype(BF)
    joined = joined.reshape(chips * columns, basis // columns, tile)
    pieces = lax.all_to_all(
        joined, ("mat", "pts"), 0, 0, tiled=True, axis_index_groups=same_core
    )
    return (summed(pieces).T, centre_features)


def solution(mesh):
    return jax.shard_map(
        shards,
        mesh=mesh,
        in_specs=(
            P(("mat", "pts"), None, None),
            P(("mat", "pts"), None),
            P("mat", None),
            P(("mat", "pts"), None, None),
            P(("mat", "pts"), None),
            P(("mat", "pts"), None),
            P(), P(), P(), P(), P(), P(), P(), P(),
        ),
        out_specs=(P("mat", "pts"), P("pts", None)),
        check_vma=False,
    )
```

```python
import functools
import math

import jax
import jax.numpy as jnp
from jax import lax
from jax.experimental import pallas as pl
from jax.experimental.pallas import tpu as pltpu
from jax.sharding import PartitionSpec as P

BF = jnp.bfloat16
F32 = jnp.float32
LANES = (((1,), (1,)), ((), ()))
MB = 1 << 20
CENT_DEV = 16


def whole(shape):
    return pl.BlockSpec(shape, lambda *_: (0,) * len(shape))


def in_hbm(x):
    return pltpu.with_memory_space_constraint(x, pltpu.HBM)


def silu(v):
    return v / (1.0 + jnp.exp(-v))


def one_hot(ids_row, centres):
    rows = lax.broadcasted_iota(jnp.int32, (centres, ids_row.shape[1]), 0)
    return (rows == ids_row).astype(F32).astype(BF)


def transpose_kernel(x_ref, o_ref):
    o_ref[0] = x_ref[0].T


def transposed(x, chunk):
    batches, points, orbitals = x.shape
    return pl.pallas_call(
        transpose_kernel,
        grid=(batches, points // chunk),
        in_specs=[pl.BlockSpec((1, chunk, orbitals), lambda b, r: (b, r, 0))],
        out_specs=pl.BlockSpec((1, orbitals, chunk), lambda b, r: (b, 0, r)),
        out_shape=jax.ShapeDtypeStruct((batches, orbitals, points), x.dtype),
        compiler_params=pltpu.CompilerParams(vmem_limit_bytes=16 * MB),
        cost_estimate=pl.CostEstimate(
            flops=0, bytes_accessed=4 * x.size, transcendentals=0
        ),
    )(in_hbm(x))


def sum_kernel(x_ref, o_ref):
    total = jnp.sum(x_ref[...].astype(F32), axis=0).astype(o_ref.dtype)
    o_ref[...] = jnp.broadcast_to(total, o_ref.shape)


def summed(x, copies=(), kind=BF):
    return pl.pallas_call(
        sum_kernel,
        out_shape=jax.ShapeDtypeStruct((*copies, *x.shape[1:]), kind),
        compiler_params=pltpu.CompilerParams(vmem_limit_bytes=8 * MB),
    )(x)


def place_slabs(pos_ref, chips, slabs, table_ref):
    core, z = pos_ref[0], pos_ref[2]
    half = table_ref.shape[1] // 2
    places = [(0, 0), (chips - 1, 0), (1, 0), (2, 0), (2, half)]
    for side in range(2):
        for k, (shift, start) in enumerate(places):
            slot = 2 * lax.rem(z + shift, chips) + (core if side == 0 else 1 - core)
            slab = slabs[side * len(places) + k]
            table_ref[slot, start : start + slab.shape[0], :] = slab[...]


def density_kernel(
    tile, chunk, chips, tid_ref, pos_ref, *refs
):
    slabs, refs = refs[:10], refs[10:]
    density_body(tile, chunk, chips, tid_ref, pos_ref, slabs, *refs)


def density_body(
    tile, chunk, chips, tid_ref, pos_ref, slabs, x_ref, desc_ref, w_ref, ids_ref, scale_ref,
    dens_ref, sum_ref, table_ref, panel_ref, acc_ref,
):
    b = pl.program_id(0)
    points, orbitals = x_ref.shape[1:]
    per_batch = orbitals // tile
    feats = desc_ref.shape[1]
    centres = 2 * sum_ref.shape[2]

    @pl.when(b == 0)
    def _():
        place_slabs(pos_ref, chips, slabs, table_ref)

    for i in range(per_batch):
        ti = tid_ref[b, i]
        for j in range(per_batch):
            tj = tid_ref[b, j]
            panel_ref[i * tile : (i + 1) * tile, j * tile : (j + 1) * tile] = table_ref[
                ti, :, pl.ds(pl.multiple_of(tj * tile, tile), tile)
            ]

    gathered = jnp.zeros(acc_ref.shape[1:], F32)
    for r in range(points // chunk):
        at = slice(r * chunk, (r + 1) * chunk)
        xt = x_ref[0, at, :].T
        q = jnp.dot(panel_ref[...], xt, preferred_element_type=F32)
        dens = jnp.sum(xt.astype(F32) * q, axis=0, keepdims=True)
        dens_ref[pl.ds(b, 1), at] = dens
        f = silu(dens * scale_ref[...] + desc_ref[0, :, at].astype(F32))
        f = f * w_ref[pl.ds(b, 1), at]
        high = f.astype(BF)
        low = (f - high.astype(F32)).astype(BF)
        both = jnp.concatenate([high, low], axis=0)
        hot = one_hot(ids_ref[pl.ds(b, 1), at], centres)
        gathered += lax.dot_general(both, hot, LANES, preferred_element_type=F32)
    acc_ref[b] = gathered

    @pl.when(b == pl.num_programs(0) - 1)
    def _():
        total = jnp.sum(acc_ref[...], axis=0)
        total = (total[:feats] + total[feats:]).astype(sum_ref.dtype)
        side = sum_ref.shape[2]
        for m in range(sum_ref.shape[0]):
            sum_ref[m] = total[:, (m % 2) * side : (m % 2 + 1) * side]


def potential_kernel(
    tile, chunk, factor, tid_ref, pos_ref, sum_ref, sum_ref_too, gain_ref, w1_ref, b1_ref, w2_ref, b2_ref, w3_ref,
    b3_ref, dens_ref, desc_ref, w_ref, ids_ref, xt_ref, x_ref, own_ref, other_ref, cf_ref,
    cft_ref, cfall_ref, wt_ref, acc_ref,
):
    b = pl.program_id(0)
    orbitals, points = xt_ref.shape[1:]
    per_batch = orbitals // tile
    centres = cft_ref.shape[1]
    mine = cf_ref.shape[0]

    @pl.when(b == 0)
    def _():
        acc_ref[...] = jnp.zeros_like(acc_ref)
        even = pos_ref[0] == 0
        here, there = sum_ref[...], sum_ref_too[...]
        total = jnp.concatenate(
            [jnp.where(even, here, there), jnp.where(even, there, here)], axis=1
        )
        inverse = lax.rsqrt(jnp.mean(total * total, axis=0, keepdims=True) + 1e-05)
        normed = ((total * inverse).T * gain_ref[...]).astype(BF)
        one = silu(
            jnp.dot(normed, w1_ref[...], preferred_element_type=F32) + b1_ref[...]
        ).astype(BF)
        two = silu(
            jnp.dot(one, w2_ref[...], preferred_element_type=F32) + b2_ref[...]
        ).astype(BF)
        feats = lax.dot_general(two, w3_ref[...], LANES, preferred_element_type=F32) + b3_ref[...]
        cfall_ref[...] = feats
        cf_ref[...] = cfall_ref[pl.ds(pl.multiple_of(pos_ref[1] * mine, 8), mine), :].astype(BF)
        cft_ref[...] = feats.T.astype(BF)

    for r in range(points // chunk):
        at = slice(r * chunk, (r + 1) * chunk)
        hot = one_hot(ids_ref[pl.ds(b, 1), at], centres)
        nearest = jnp.dot(cft_ref[...], hot, preferred_element_type=F32)
        inner = jnp.sum(nearest * desc_ref[0, :, at].astype(F32), axis=0, keepdims=True)
        v = w_ref[pl.ds(b, 1), at] * dens_ref[pl.ds(b, 1), at] * inner * factor
        wt_ref[:, at] = (v * xt_ref[0, :, at].astype(F32)).astype(BF)
    for i in range(per_batch):
        rows = slice(i * tile, (i + 1) * tile)
        block = jnp.dot(wt_ref[rows, :], x_ref[0], preferred_element_type=F32)
        for j in range(per_batch):
            acc_ref[tid_ref[b, i], tid_ref[b, j]] += block[:, j * tile : (j + 1) * tile]

    @pl.when(b == pl.num_programs(0) - 1)
    def _():
        core = pos_ref[0]
        for z in range(own_ref.shape[0]):
            for i in range(own_ref.shape[1]):
                own_ref[z, i] = acc_ref[i, 2 * z + core]
                other_ref[z, i] = acc_ref[i, 2 * z + 1 - core].astype(BF)


def shards(
    basis_values, tile_ids, density_matrix, descriptors, grid_weights, centre_ids, density_scale,
    norm_gain, w_first, b_first, w_second, b_second, w_third, b_third,
):
    batches, points, orbitals = basis_values.shape
    per_batch = tile_ids.shape[1]
    tile = orbitals // per_batch
    basis = density_matrix.shape[1]
    tiles = basis // tile
    feats = descriptors.shape[2]
    mats = lax.axis_size("mat")
    columns = lax.axis_size("pts")
    chips = mats // 2
    mine = CENT_DEV
    centres = mine * columns
    chunk = 512
    here, there = lax.axis_index("mat"), lax.axis_index("pts")
    pos = jnp.stack([here % 2, there, here // 2]).astype(jnp.int32)
    swap = [(i, i ^ 1) for i in range(mats)]
    up = [(i, (i + 2) % mats) for i in range(mats)]
    down = [(i, (i - 2) % mats) for i in range(mats)]
    across = [(i, (i + 4) % mats) for i in range(mats)]
    same_core = [
        [m * columns + p for m in range(c, mats, 2) for p in range(columns)] for c in range(2)
    ]
    desc = jnp.swapaxes(descriptors, 1, 2)
    scale = density_scale.reshape(feats, 1)

    top = lax.ppermute(density_matrix[: tile // 2], "mat", across)
    bottom = lax.ppermute(density_matrix[tile // 2 :], "mat", across)
    below = lax.ppermute(density_matrix, "mat", up)
    above = lax.ppermute(density_matrix, "mat", down)
    xt = transposed(basis_values, points)
    top, bottom, below, above, xt = lax.optimization_barrier((top, bottom, below, above, xt))
    slabs = [density_matrix, below, above, top, bottom]
    slabs += [lax.ppermute(slab, "mat", swap) for slab in slabs]

    density, partial = pl.pallas_call(
        functools.partial(density_kernel, tile, chunk, chips),
        grid_spec=pltpu.PrefetchScalarGridSpec(
            num_scalar_prefetch=2,
            grid=(batches,),
            in_specs=[
                *[whole(slab.shape) for slab in slabs],
                pl.BlockSpec((1, points, orbitals), lambda b, *_: (b, 0, 0)),
                pl.BlockSpec((1, feats, points), lambda b, *_: (b, 0, 0)),
                whole((batches, points)),
                whole((batches, points)),
                whole((feats, 1)),
            ],
            out_specs=[whole((batches, points)), whole((mats, feats, centres // 2))],
            scratch_shapes=[
                pltpu.VMEM((tiles, tile, basis), BF),
                pltpu.VMEM((orbitals, orbitals), BF),
                pltpu.VMEM((batches, 2 * feats, centres), F32),
            ],
        ),
        out_shape=[
            jax.ShapeDtypeStruct((batches, points), F32),
            jax.ShapeDtypeStruct((mats, feats, centres // 2), BF),
        ],
        compiler_params=pltpu.CompilerParams(vmem_limit_bytes=16 * MB),
        cost_estimate=pl.CostEstimate(
            flops=2 * batches * points * orbitals * orbitals,
            bytes_accessed=2 * basis_values.size,
            transcendentals=descriptors.size,
        ),
    )(
        tile_ids, pos, *slabs, in_hbm(basis_values), desc, grid_weights, centre_ids, scale,
    )

    first = summed(lax.all_to_all(partial, "mat", 0, 0, tiled=True), (columns,))
    mine_sum = summed(lax.all_to_all(first, "pts", 0, 0, tiled=True), kind=F32)
    their_sum = lax.ppermute(mine_sum, "mat", swap)

    all_batches = batches * mats * columns
    factor = tiles / (per_batch * math.sqrt(points * feats * all_batches))
    hidden = w_first.shape[1]
    own, other, centre_features = pl.pallas_call(
        functools.partial(potential_kernel, tile, chunk, factor),
        grid_spec=pltpu.PrefetchScalarGridSpec(
            num_scalar_prefetch=2,
            grid=(batches,),
            in_specs=[
                whole((feats, centres // 2)),
                whole((feats, centres // 2)),
                whole((1, feats)),
                whole((feats, hidden)),
                whole((1, hidden)),
                whole((hidden, hidden)),
                whole((1, hidden)),
                whole((feats, hidden)),
                whole((1, feats)),
                whole((batches, points)),
                pl.BlockSpec((1, feats, points), lambda b, *_: (b, 0, 0)),
                whole((batches, points)),
                whole((batches, points)),
                pl.BlockSpec((1, orbitals, points), lambda b, *_: (b, 0, 0)),
                pl.BlockSpec((1, points, orbitals), lambda b, *_: (b, 0, 0)),
            ],
            out_specs=[
                whole((chips, tiles, tile, tile)),
                whole((chips, tiles, tile, tile)),
                whole((mine, feats)),
            ],
            scratch_shapes=[
                pltpu.VMEM((feats, centres), BF),
                pltpu.VMEM((centres, feats), F32),
                pltpu.VMEM((orbitals, points), BF),
                pltpu.VMEM((tiles, tiles, tile, tile), F32),
            ],
        ),
        out_shape=[
            jax.ShapeDtypeStruct((chips, tiles, tile, tile), F32),
            jax.ShapeDtypeStruct((chips, tiles, tile, tile), BF),
            jax.ShapeDtypeStruct((mine, feats), BF),
        ],
        compiler_params=pltpu.CompilerParams(vmem_limit_bytes=28 * MB),
        cost_estimate=pl.CostEstimate(
            flops=2 * batches * points * orbitals * orbitals,
            bytes_accessed=4 * basis_values.size,
            transcendentals=2 * centres * hidden,
        ),
    )(
        tile_ids, pos, mine_sum, their_sum, norm_gain.reshape(1, feats), w_first, b_first.reshape(1, hidden),
        w_second, b_second.reshape(1, hidden), w_third.T, b_third.reshape(1, feats), density, desc,
        grid_weights, centre_ids, xt, basis_values,
    )

    joined = (own + lax.ppermute(other, "mat", swap).astype(F32)).astype(BF)
    joined = joined.reshape(chips * columns, basis // columns, tile)
    pieces = lax.all_to_all(
        joined, ("mat", "pts"), 0, 0, tiled=True, axis_index_groups=same_core
    )
    return (summed(pieces).T, centre_features)


def solution(mesh):
    return jax.shard_map(
        shards,
        mesh=mesh,
        in_specs=(
            P(("mat", "pts"), None, None),
            P(("mat", "pts"), None),
            P("mat", None),
            P(("mat", "pts"), None, None),
            P(("mat", "pts"), None),
            P(("mat", "pts"), None),
            P(), P(), P(), P(), P(), P(), P(), P(),
        ),
        out_specs=(P("mat", "pts"), P("pts", None)),
        check_vma=False,
    )
```

```python
import functools
import math

import jax
import jax.numpy as jnp
from jax import lax
from jax.experimental import pallas as pl
from jax.experimental.pallas import tpu as pltpu
from jax.sharding import PartitionSpec as P

BF = jnp.bfloat16
F32 = jnp.float32
LANES = (((1,), (1,)), ((), ()))
MB = 1 << 20
CENT_DEV = 16


def whole(shape):
    return pl.BlockSpec(shape, lambda *_: (0,) * len(shape))


def in_hbm(x):
    return pltpu.with_memory_space_constraint(x, pltpu.HBM)


def silu(v):
    return v / (1.0 + jnp.exp(-v))


def one_hot(ids_row, centres):
    rows = lax.broadcasted_iota(jnp.int32, (centres, ids_row.shape[1]), 0)
    return (rows == ids_row).astype(F32).astype(BF)


def transpose_kernel(x_ref, o_ref):
    o_ref[0] = x_ref[0].T


def transposed(x, chunk):
    batches, points, orbitals = x.shape
    return pl.pallas_call(
        transpose_kernel,
        grid=(batches, points // chunk),
        in_specs=[pl.BlockSpec((1, chunk, orbitals), lambda b, r: (b, r, 0))],
        out_specs=pl.BlockSpec((1, orbitals, chunk), lambda b, r: (b, 0, r)),
        out_shape=pltpu.HBM((batches, orbitals, points), x.dtype),
        compiler_params=pltpu.CompilerParams(vmem_limit_bytes=16 * MB),
        cost_estimate=pl.CostEstimate(
            flops=0, bytes_accessed=4 * x.size, transcendentals=0
        ),
    )(in_hbm(x))


def sum_kernel(x_ref, o_ref):
    total = jnp.sum(x_ref[...].astype(F32), axis=0).astype(o_ref.dtype)
    o_ref[...] = jnp.broadcast_to(total, o_ref.shape)


def summed(x, copies=(), kind=BF):
    return pl.pallas_call(
        sum_kernel,
        out_shape=jax.ShapeDtypeStruct((*copies, *x.shape[1:]), kind),
        compiler_params=pltpu.CompilerParams(vmem_limit_bytes=8 * MB),
    )(x)


def place_slabs(pos_ref, chips, slabs, table_ref):
    core, z = pos_ref[0], pos_ref[2]
    half = table_ref.shape[1] // 2
    places = [(0, 0), (chips - 1, 0), (1, 0), (2, 0), (2, half)]
    for side in range(2):
        for k, (shift, start) in enumerate(places):
            slot = 2 * lax.rem(z + shift, chips) + (core if side == 0 else 1 - core)
            slab = slabs[side * len(places) + k]
            table_ref[slot, start : start + slab.shape[0], :] = slab[...]


def density_kernel(
    tile, chunk, chips, tid_ref, pos_ref, *refs
):
    slabs, refs = refs[:10], refs[10:]
    density_body(tile, chunk, chips, tid_ref, pos_ref, slabs, *refs)


def density_body(
    tile, chunk, chips, tid_ref, pos_ref, slabs, x_ref, desc_ref, w_ref, ids_ref, scale_ref,
    dens_ref, sum_ref, table_ref, panel_ref, acc_ref,
):
    b = pl.program_id(0)
    points, orbitals = x_ref.shape[1:]
    per_batch = orbitals // tile
    feats = desc_ref.shape[1]
    centres = 2 * sum_ref.shape[2]

    @pl.when(b == 0)
    def _():
        place_slabs(pos_ref, chips, slabs, table_ref)

    for i in range(per_batch):
        ti = tid_ref[b, i]
        for j in range(per_batch):
            tj = tid_ref[b, j]
            panel_ref[i * tile : (i + 1) * tile, j * tile : (j + 1) * tile] = table_ref[
                ti, :, pl.ds(pl.multiple_of(tj * tile, tile), tile)
            ]

    gathered = jnp.zeros(acc_ref.shape[1:], F32)
    for r in range(points // chunk):
        at = slice(r * chunk, (r + 1) * chunk)
        xt = x_ref[0, at, :].T
        q = jnp.dot(panel_ref[...], xt, preferred_element_type=F32)
        dens = jnp.sum(xt.astype(F32) * q, axis=0, keepdims=True)
        dens_ref[pl.ds(b, 1), at] = dens
        f = silu(dens * scale_ref[...] + desc_ref[0, :, at].astype(F32))
        f = f * w_ref[pl.ds(b, 1), at]
        high = f.astype(BF)
        low = (f - high.astype(F32)).astype(BF)
        both = jnp.concatenate([high, low], axis=0)
        hot = one_hot(ids_ref[pl.ds(b, 1), at], centres)
        gathered += lax.dot_general(both, hot, LANES, preferred_element_type=F32)
    acc_ref[b] = gathered

    @pl.when(b == pl.num_programs(0) - 1)
    def _():
        total = jnp.sum(acc_ref[...], axis=0)
        total = (total[:feats] + total[feats:]).astype(sum_ref.dtype)
        side = sum_ref.shape[2]
        for m in range(sum_ref.shape[0]):
            sum_ref[m] = total[:, (m % 2) * side : (m % 2 + 1) * side]


def potential_kernel(
    tile, chunk, factor, tid_ref, pos_ref, sum_ref, sum_ref_too, gain_ref, w1_ref, b1_ref, w2_ref, b2_ref, w3_ref,
    b3_ref, dens_ref, desc_ref, w_ref, ids_ref, xt_ref, x_ref, own_ref, other_ref, cf_ref,
    cft_ref, cfall_ref, wt_ref, acc_ref,
):
    b = pl.program_id(0)
    orbitals, points = xt_ref.shape[1:]
    per_batch = orbitals // tile
    centres = cft_ref.shape[1]
    mine = cf_ref.shape[0]

    @pl.when(b == 0)
    def _():
        acc_ref[...] = jnp.zeros_like(acc_ref)
        even = pos_ref[0] == 0
        here, there = sum_ref[...], sum_ref_too[...]
        total = jnp.concatenate(
            [jnp.where(even, here, there), jnp.where(even, there, here)], axis=1
        )
        inverse = lax.rsqrt(jnp.mean(total * total, axis=0, keepdims=True) + 1e-05)
        normed = ((total * inverse).T * gain_ref[...]).astype(BF)
        one = silu(
            jnp.dot(normed, w1_ref[...], preferred_element_type=F32) + b1_ref[...]
        ).astype(BF)
        two = silu(
            jnp.dot(one, w2_ref[...], preferred_element_type=F32) + b2_ref[...]
        ).astype(BF)
        feats = lax.dot_general(two, w3_ref[...], LANES, preferred_element_type=F32) + b3_ref[...]
        cfall_ref[...] = feats
        cf_ref[...] = cfall_ref[pl.ds(pl.multiple_of(pos_ref[1] * mine, 8), mine), :].astype(BF)
        cft_ref[...] = feats.T.astype(BF)

    for r in range(points // chunk):
        at = slice(r * chunk, (r + 1) * chunk)
        hot = one_hot(ids_ref[pl.ds(b, 1), at], centres)
        nearest = jnp.dot(cft_ref[...], hot, preferred_element_type=F32)
        inner = jnp.sum(nearest * desc_ref[0, :, at].astype(F32), axis=0, keepdims=True)
        v = w_ref[pl.ds(b, 1), at] * dens_ref[pl.ds(b, 1), at] * inner * factor
        wt_ref[:, at] = (v * xt_ref[0, :, at].astype(F32)).astype(BF)
    for i in range(per_batch):
        rows = slice(i * tile, (i + 1) * tile)
        block = jnp.dot(wt_ref[rows, :], x_ref[0], preferred_element_type=F32)
        for j in range(per_batch):
            acc_ref[tid_ref[b, i], tid_ref[b, j]] += block[:, j * tile : (j + 1) * tile]

    @pl.when(b == pl.num_programs(0) - 1)
    def _():
        core = pos_ref[0]
        for z in range(own_ref.shape[0]):
            for i in range(own_ref.shape[1]):
                own_ref[z, i] = acc_ref[i, 2 * z + core]
                other_ref[z, i] = acc_ref[i, 2 * z + 1 - core].astype(BF)


def shards(
    basis_values, tile_ids, density_matrix, descriptors, grid_weights, centre_ids, density_scale,
    norm_gain, w_first, b_first, w_second, b_second, w_third, b_third,
):
    batches, points, orbitals = basis_values.shape
    per_batch = tile_ids.shape[1]
    tile = orbitals // per_batch
    basis = density_matrix.shape[1]
    tiles = basis // tile
    feats = descriptors.shape[2]
    mats = lax.axis_size("mat")
    columns = lax.axis_size("pts")
    chips = mats // 2
    mine = CENT_DEV
    centres = mine * columns
    chunk = 512
    here, there = lax.axis_index("mat"), lax.axis_index("pts")
    pos = jnp.stack([here % 2, there, here // 2]).astype(jnp.int32)
    swap = [(i, i ^ 1) for i in range(mats)]
    up = [(i, (i + 2) % mats) for i in range(mats)]
    down = [(i, (i - 2) % mats) for i in range(mats)]
    across = [(i, (i + 4) % mats) for i in range(mats)]
    same_core = [
        [m * columns + p for m in range(c, mats, 2) for p in range(columns)] for c in range(2)
    ]
    desc = jnp.swapaxes(descriptors, 1, 2)
    scale = density_scale.reshape(feats, 1)

    top = lax.ppermute(density_matrix[: tile // 2], "mat", across)
    bottom = lax.ppermute(density_matrix[tile // 2 :], "mat", across)
    below = lax.ppermute(density_matrix, "mat", up)
    above = lax.ppermute(density_matrix, "mat", down)
    xt = transposed(basis_values, points)
    top, bottom, below, above, xt = lax.optimization_barrier((top, bottom, below, above, xt))
    slabs = [density_matrix, below, above, top, bottom]
    slabs += [lax.ppermute(slab, "mat", swap) for slab in slabs]

    density, partial = pl.pallas_call(
        functools.partial(density_kernel, tile, points, chips),
        grid_spec=pltpu.PrefetchScalarGridSpec(
            num_scalar_prefetch=2,
            grid=(batches,),
            in_specs=[
                *[whole(slab.shape) for slab in slabs],
                pl.BlockSpec((1, points, orbitals), lambda b, *_: (b, 0, 0)),
                pl.BlockSpec((1, feats, points), lambda b, *_: (b, 0, 0)),
                whole((batches, points)),
                whole((batches, points)),
                whole((feats, 1)),
            ],
            out_specs=[whole((batches, points)), whole((mats, feats, centres // 2))],
            scratch_shapes=[
                pltpu.VMEM((tiles, tile, basis), BF),
                pltpu.VMEM((orbitals, orbitals), BF),
                pltpu.VMEM((batches, 2 * feats, centres), F32),
            ],
        ),
        out_shape=[
            jax.ShapeDtypeStruct((batches, points), F32),
            jax.ShapeDtypeStruct((mats, feats, centres // 2), BF),
        ],
        compiler_params=pltpu.CompilerParams(vmem_limit_bytes=16 * MB),
        cost_estimate=pl.CostEstimate(
            flops=2 * batches * points * orbitals * orbitals,
            bytes_accessed=2 * basis_values.size,
            transcendentals=descriptors.size,
        ),
    )(
        tile_ids, pos, *slabs, in_hbm(basis_values), desc, grid_weights, centre_ids, scale,
    )

    first = summed(lax.all_to_all(partial, "mat", 0, 0, tiled=True), (columns,))
    mine_sum = summed(lax.all_to_all(first, "pts", 0, 0, tiled=True), kind=F32)
    their_sum = lax.ppermute(mine_sum, "mat", swap)

    all_batches = batches * mats * columns
    factor = tiles / (per_batch * math.sqrt(points * feats * all_batches))
    hidden = w_first.shape[1]
    own, other, centre_features = pl.pallas_call(
        functools.partial(potential_kernel, tile, chunk, factor),
        grid_spec=pltpu.PrefetchScalarGridSpec(
            num_scalar_prefetch=2,
            grid=(batches,),
            in_specs=[
                whole((feats, centres // 2)),
                whole((feats, centres // 2)),
                whole((1, feats)),
                whole((feats, hidden)),
                whole((1, hidden)),
                whole((hidden, hidden)),
                whole((1, hidden)),
                whole((feats, hidden)),
                whole((1, feats)),
                whole((batches, points)),
                pl.BlockSpec((1, feats, points), lambda b, *_: (b, 0, 0)),
                whole((batches, points)),
                whole((batches, points)),
                pl.BlockSpec((1, orbitals, points), lambda b, *_: (b, 0, 0)),
                pl.BlockSpec((1, points, orbitals), lambda b, *_: (b, 0, 0)),
            ],
            out_specs=[
                whole((chips, tiles, tile, tile)),
                whole((chips, tiles, tile, tile)),
                whole((mine, feats)),
            ],
            scratch_shapes=[
                pltpu.VMEM((feats, centres), BF),
                pltpu.VMEM((centres, feats), F32),
                pltpu.VMEM((orbitals, points), BF),
                pltpu.VMEM((tiles, tiles, tile, tile), F32),
            ],
        ),
        out_shape=[
            jax.ShapeDtypeStruct((chips, tiles, tile, tile), F32),
            jax.ShapeDtypeStruct((chips, tiles, tile, tile), BF),
            jax.ShapeDtypeStruct((mine, feats), BF),
        ],
        compiler_params=pltpu.CompilerParams(vmem_limit_bytes=28 * MB),
        cost_estimate=pl.CostEstimate(
            flops=2 * batches * points * orbitals * orbitals,
            bytes_accessed=4 * basis_values.size,
            transcendentals=2 * centres * hidden,
        ),
    )(
        tile_ids, pos, mine_sum, their_sum, norm_gain.reshape(1, feats), w_first, b_first.reshape(1, hidden),
        w_second, b_second.reshape(1, hidden), w_third.T, b_third.reshape(1, feats), density, desc,
        grid_weights, centre_ids, xt, basis_values,
    )

    joined = (own + lax.ppermute(other, "mat", swap).astype(F32)).astype(BF)
    joined = joined.reshape(chips * columns, basis // columns, tile)
    pieces = lax.all_to_all(
        joined, ("mat", "pts"), 0, 0, tiled=True, axis_index_groups=same_core
    )
    return (summed(pieces).T, centre_features)


def solution(mesh):
    return jax.shard_map(
        shards,
        mesh=mesh,
        in_specs=(
            P(("mat", "pts"), None, None),
            P(("mat", "pts"), None),
            P("mat", None),
            P(("mat", "pts"), None, None),
            P(("mat", "pts"), None),
            P(("mat", "pts"), None),
            P(), P(), P(), P(), P(), P(), P(), P(),
        ),
        out_specs=(P("mat", "pts"), P("pts", None)),
        check_vma=False,
    )
```
